32 devices in a mesh: gx: 8 (over z, core), gy: 2 (over x), ga: 2 (over y).
Axes of the slice: x: 2, y: 2, z: 4, core: 2. Of those that a mesh axis runs over, the one named last changes fastest.
Arguments:
- samples: bfloat16 [16, 64, 32, 512], P('ga', 'gx', 'gy'), parts along dimension 0, may hold values from -6 to 6
- model_prev: bfloat16 [16, 64, 32, 512], P('ga', 'gx', 'gy'), parts along dimension 0, may hold values from -6 to 6
- threshold: float32 [64, 32], P('gx', 'gy'), may hold values from 0.1 to 1
- support: int32 [64, 32, 256], P('gx', 'gy'), may hold values from 0 to 511
- sample_basis: bfloat16 [512, 64], replicated, may hold values from -0.25 to 0.25
- eval_basis: bfloat16 [64, 512], replicated, may hold values from -0.25 to 0.25
- transfer_x: bfloat16 [8, 8, 64, 64], replicated, may hold values from -0.25 to 0.25
- transfer_y: bfloat16 [2, 2, 64, 64], replicated, may hold values from -0.5 to 0.5
Outputs:
- model_next: float32 [16, 64, 32, 512], P('ga', 'gx', 'gy'), parts along dimension 0
- residual: bfloat16 [16, 64, 32, 512], P('ga', 'gx', 'gy'), parts along dimension 0
The draws below stay inside these ranges and needn't reach their ends.
There are 2 independent parts, one for each index of `ga`. The reference program is written for one: setup_inputs(seed, part) draws one part's arguments, and reference() takes and returns one part's arrays. A program takes and returns all parts, laid end to end along the dimension named above; an argument that names none is the same for every part. Nothing has to cross between parts.
All inputs are finite; a program needn't handle non-finite values.
Results may differ from the reference program's by a relative error of at most 0.015.
Values may be sent and summed in bfloat16 or wider, within the bound.
No kernel may reach another device: no remote copies, remote signals or barrier semaphores. Data moves between devices by JAX's collectives and lax.ppermute only.
A program may use at most 64 MiB of HBM per device.

```python
import jax
import jax.numpy as jnp

G = 8
K = 64
LX = 8
LY = 16
SB = 512
RB = 512
NSUP = 256
BX = 64
BY = 32
N_GX = 8
N_GY = 2


def touch_ends(array, own_key, least, largest):
    index_at = [jax.random.randint(jax.random.fold_in(own_key, axis), (), 0, length) for axis, length in enumerate(array.shape)]
    widest = array.shape.index(max(array.shape))
    neighbour = index_at[:widest] + [(index_at[widest] + 1) % array.shape[widest]] + index_at[widest + 1:]
    return array.at[tuple(index_at)].set(least).at[tuple(neighbour)].set(largest)


def shard_levels(rng, shape, split, smallest, top_value):
    factor_of, own = 1.0, jax.random.fold_in(rng, 6)
    for position, shards_of in split:
        draws = jnp.exp(jax.random.uniform(jax.random.fold_in(own, position), (shards_of,), jnp.float32, smallest / len(split), top_value / len(split)))
        factor_of = factor_of * jnp.repeat(draws, shape[position] // shards_of).reshape([-1 if axis == position else 1 for axis in range(len(shape))])
    return factor_of


def bell_draw(stream_key, shape, deviation, reach, pieces=(), kind=jnp.bfloat16):
    drawn = deviation * jax.random.normal(stream_key, shape, jnp.float32)
    if pieces:
        drawn = drawn * shard_levels(stream_key, shape, pieces, -0.22, 0.18)
    return jnp.clip(drawn, -reach, reach).astype(kind)


def setup_inputs(seed: int = 0, part: int = 0) -> dict:
    key_list = jax.random.split(jax.random.key(seed), 9)
    own_keys = jax.random.split(jax.random.fold_in(key_list[8], part), 9)
    samples = bell_draw(own_keys[0], (G, BX, BY, SB), 1.0, 6.0, ((1, 8), (2, 2)))
    model_prev = bell_draw(own_keys[1], (G, BX, BY, RB), 1.0, 6.0, ((1, 8), (2, 2)))
    threshold = jnp.clip(0.1 + 0.9 * jax.random.uniform(key_list[2], (BX, BY), jnp.float32) ** shard_levels(key_list[2], (BX, BY), ((0, 8), (1, 2)), -0.2, 0.2), 0.1, 1.0)
    support = touch_ends(jax.random.randint(key_list[3], (BX, BY, NSUP), 0, RB), jax.random.fold_in(key_list[3], 1), 0, RB - 1).astype(jnp.int32)
    sample_basis = bell_draw(key_list[4], (SB, K), SB ** -0.5, 0.25)
    eval_basis = bell_draw(key_list[5], (K, RB), RB ** -0.5, 0.25)
    transfer_x = bell_draw(key_list[6], (N_GX, N_GX, K, K), (N_GX * K) ** -0.5, 0.25)
    transfer_y = bell_draw(key_list[7], (N_GY, N_GY, K, K), (N_GY * K) ** -0.5, 0.5)
    return {"samples": samples, "model_prev": model_prev, "threshold": threshold, "support": support, "sample_basis": sample_basis, "eval_basis": eval_basis, "transfer_x": transfer_x, "transfer_y": transfer_y}


def level_mix_x(coeffs, tables):
    shaped = coeffs.astype(jnp.float32).reshape(G, N_GX, LX, BY, K)
    mixed = jnp.einsum('gslyk,askq->galyq', shaped, tables.astype(jnp.float32))
    return mixed.reshape(G, BX, BY, K)


def level_mix_y(coeffs, tables):
    shaped = coeffs.astype(jnp.float32).reshape(G, BX, N_GY, LY, K)
    mixed = jnp.einsum('gxsmk,askq->gxamq', shaped, tables.astype(jnp.float32))
    return mixed.reshape(G, BX, BY, K)


def reference(samples, model_prev, threshold, support, sample_basis, eval_basis, transfer_x, transfer_y):
    flipped_x = jnp.transpose(transfer_x, (1, 0, 3, 2))
    flipped_y = jnp.transpose(transfer_y, (1, 0, 3, 2))
    top = jnp.einsum('gxyr,kr->gxyk', model_prev.astype(jnp.float32), eval_basis.astype(jnp.float32)).astype(jnp.bfloat16)
    middle = level_mix_y(top, flipped_y).astype(jnp.bfloat16)
    low = level_mix_x(middle, flipped_x).astype(jnp.bfloat16)
    predicted = jnp.einsum('gxyk,tk->gxyt', low.astype(jnp.float32), sample_basis.astype(jnp.float32))
    residual = (samples.astype(jnp.float32) - predicted).astype(jnp.bfloat16)
    back_low = jnp.einsum('gxyt,tk->gxyk', residual.astype(jnp.float32), sample_basis.astype(jnp.float32)).astype(jnp.bfloat16)
    back_mid = level_mix_x(back_low, transfer_x).astype(jnp.bfloat16)
    back_top = level_mix_y(back_mid, transfer_y).astype(jnp.bfloat16)
    update = jnp.einsum('gxyk,kr->gxyr', back_top.astype(jnp.float32), eval_basis.astype(jnp.float32))
    stepped = model_prev.astype(jnp.float32) + update
    shrunk = jnp.sign(stepped) * jnp.maximum(jnp.abs(stepped) - threshold[None, :, :, None], 0.0)
    row_index = jnp.arange(BX, dtype=jnp.int32)[:, None, None]
    col_index = jnp.arange(BY, dtype=jnp.int32)[None, :, None]
    support_mask = jnp.zeros((BX, BY, RB), jnp.float32).at[row_index, col_index, support].set(1.0)
    return shrunk * support_mask[None], residual
```

```python
import functools

import jax
import jax.numpy as jnp
from jax import lax
from jax.experimental import pallas as pl
from jax.experimental.pallas import tpu as pltpu
from jax.sharding import PartitionSpec as P


CHUNKS = 1
F32 = jnp.float32
BF16 = jnp.bfloat16


def mm(a, b):
    return lax.dot_general(a, b, (((1,), (0,)), ((), ())), preferred_element_type=F32)


def mm_nt(a, b):
    return lax.dot_general(a, b, (((1,), (1,)), ((), ())), preferred_element_type=F32)


def swap(x, axes, mesh_shape, masks):
    sizes = [mesh_shape[axis] for axis in axes]
    total = 1
    for size in sizes:
        total *= size
    pairs = []
    for source in range(total):
        rest, coords = source, []
        for size in reversed(sizes):
            coords.append(rest % size)
            rest //= size
        coords.reverse()
        target = 0
        for coord, mask, size in zip(coords, masks, sizes):
            target = target * size + (coord ^ mask)
        pairs.append((source, target))
    return lax.ppermute(x, axes, pairs)


def coeff_kernel(model_ref, samples_ref, eval_ref, basis_ref, out_ref):
    k = eval_ref.shape[0]
    weights = jnp.concatenate([eval_ref[...], basis_ref[...]], axis=0)
    top = mm_nt(model_ref[...], weights)
    low = mm_nt(samples_ref[...], weights)
    lane = lax.broadcasted_iota(jnp.int32, top.shape, 1)
    out_ref[...] = jnp.where(lane < k, top, low).astype(BF16)


def coefficients(model, samples, evals, basis_t):
    rows, width = model.shape
    k = evals.shape[0]
    block = min(rows, 256)
    wide = pl.BlockSpec((block, width), lambda i: (i, 0))
    whole = pl.BlockSpec((k, width), lambda i: (0, 0))
    return pl.pallas_call(
        coeff_kernel,
        grid=(rows // block,),
        in_specs=[wide, wide, whole, whole],
        out_specs=pl.BlockSpec((block, 2 * k), lambda i: (i, 0)),
        out_shape=jax.ShapeDtypeStruct((rows, 2 * k), BF16),
        cost_estimate=pl.CostEstimate(
            flops=8 * rows * width * k, bytes_accessed=4 * rows * (width + k), transcendentals=0
        ),
        name="coefficients",
    )(model, samples, evals, basis_t)


def table_kernel(n_gy, near, xt_ref, tx_ref, ty_ref, tyt_ref, basis_ref, out_ref):
    k = basis_ref.shape[0]
    own_x, own_y = lax.axis_index("gx"), lax.axis_index("gy")
    targets = (own_x, own_x ^ near)
    span = 4
    stacked = jnp.concatenate([basis_ref[...]] * span, axis=0)
    gram = mm_nt(stacked, stacked)
    row = lax.broadcasted_iota(jnp.int32, gram.shape, 0) // k
    col = lax.broadcasted_iota(jnp.int32, gram.shape, 1) // k
    gram = jnp.where(row == col, gram, 0.0).astype(BF16)
    to_targets = jnp.concatenate([xt_ref[t] for t in targets], axis=0)
    step = span * k
    weighted = jnp.concatenate(
        [
            mm(to_targets[:, i : i + step], gram).astype(BF16)
            for i in range(0, to_targets.shape[1], step)
        ],
        axis=1,
    )
    sources = jnp.concatenate([xt_ref[own_x ^ m] for m in range(near)], axis=0)
    cross = mm_nt(sources, weighted).astype(BF16)
    zero = jnp.zeros((k, k), BF16)

    def pair(block):
        return jnp.concatenate(
            [jnp.concatenate([block, zero], axis=1), jnp.concatenate([zero, block], axis=1)], axis=0
        )

    inner = [mm(cross, pair(ty_ref[own_y, m])).astype(BF16) for m in range(n_gy)]
    lane = lax.broadcasted_iota(jnp.int32, (k, 2 * k), 1)
    for m in range(near):
        source = own_x ^ m
        stacked_inner = jnp.concatenate([part[m * k : (m + 1) * k] for part in inner], axis=0)
        normal = mm(tyt_ref[...], stacked_inner)
        to_rows = jnp.concatenate([tx_ref[source, t] for t in targets], axis=0)
        from_rows = jnp.concatenate([tx_ref[t, source] for t in targets], axis=0)
        for s in range(n_gy):
            forward = mm_nt(ty_ref[s, own_y].T, to_rows)
            back = mm(from_rows, jnp.concatenate([ty_ref[own_y, s]] * 2, axis=1))
            negated = normal[s * k : (s + 1) * k]
            slot = (s ^ own_y) * near + m
            first = jnp.where(lane < k, forward, -jnp.roll(negated, k, axis=1))
            second = jnp.where(lane < k, jnp.roll(forward, k, axis=1), -negated)
            out_ref[slot, :k, : 2 * k] = first.astype(BF16)
            out_ref[slot, :k, 2 * k :] = second.astype(BF16)
            for i in range(2):
                adjoint = jnp.where(lane < k, 0.0, back[i * k : (i + 1) * k])
                out_ref[slot, k:, 2 * k * i : 2 * k * (i + 1)] = adjoint.astype(BF16)


def make_tables(n_gy, near, transfer_x, transfer_y, basis_t):
    n_gx, k = transfer_x.shape[0], transfer_x.shape[3]
    x_t = jnp.transpose(transfer_x, (0, 3, 1, 2)).reshape(n_gx, k, n_gx * k)
    y_t = jnp.transpose(transfer_y, (0, 3, 1, 2)).reshape(n_gy * k, n_gy * k)
    return pl.pallas_call(
        functools.partial(table_kernel, n_gy, near),
        out_shape=jax.ShapeDtypeStruct((n_gy * near, 2 * k, 4 * k), BF16),
        cost_estimate=pl.CostEstimate(
            flops=200000000, bytes_accessed=2000000, transcendentals=0
        ),
        name="tables",
    )(x_t, transfer_x, transfer_y, y_t, basis_t)


def mask_kernel(support_ref, threshold_ref, out_ref):
    count = out_ref.shape[1]
    picked = support_ref[...].T
    word, bit = picked >> 5, jnp.int32(1) << (picked & 31)
    words = count // 32
    index = lax.broadcasted_iota(jnp.int32, (words, picked.shape[1]), 0)
    bits = jnp.zeros(index.shape, jnp.int32)
    for j in range(picked.shape[0]):
        bits = bits | jnp.where(index == word[j : j + 1], bit[j : j + 1], 0)
    shift = lax.broadcasted_iota(jnp.int32, (32, picked.shape[1]), 0)
    flags = jnp.concatenate([(bits[w : w + 1] >> shift) & 1 for w in range(words)], axis=0)
    out_ref[...] = jnp.where(flags.T != 0, threshold_ref[...], jnp.inf)


def threshold_map(support, threshold, width):
    boxes = support.shape[0]
    return pl.pallas_call(
        mask_kernel,
        out_shape=jax.ShapeDtypeStruct((boxes, width), F32),
        cost_estimate=pl.CostEstimate(
            flops=boxes * width * 32, bytes_accessed=4 * boxes * width, transcendentals=0
        ),
        name="threshold_map",
    )(support, threshold)


def mix_kernel(count, *refs):
    tables_ref, far_ref, own_ref = refs[count:]
    k2 = refs[0].shape[1]
    gathered = jnp.concatenate([ref[...] for ref in refs[:count]], axis=1)
    tables = tables_ref[...].reshape(count * k2, 2 * k2)
    mixed = mm(gathered, tables)
    own_ref[...] = mixed[:, :k2]
    far_ref[...] = mixed[:, k2:].astype(BF16)


def mix(parts, tables):
    rows, k2 = parts[0].shape
    count = len(parts)
    block = min(rows, 256)
    spec = pl.BlockSpec((block, k2), lambda i: (i, 0))
    return pl.pallas_call(
        functools.partial(mix_kernel, count),
        grid=(rows // block,),
        in_specs=[spec] * count + [pl.BlockSpec(tables.shape, lambda i: (0, 0, 0))],
        out_specs=[spec, spec],
        out_shape=[
            jax.ShapeDtypeStruct((rows, k2), BF16),
            jax.ShapeDtypeStruct((rows, k2), F32),
        ],
        cost_estimate=pl.CostEstimate(
            flops=4 * rows * count * k2 * k2,
            bytes_accessed=2 * rows * k2 * count,
            transcendentals=0,
        ),
        name="mix",
    )(*parts, tables)


def finish_kernel(own_ref, far_ref, model_ref, samples_ref, limit_ref, eval_ref, basis_ref, next_ref, residual_ref):
    k = eval_ref.shape[0]
    both = (own_ref[...] + far_ref[...].astype(F32)).astype(BF16)
    zero = jnp.zeros(eval_ref.shape, BF16)
    predicted = mm(both, jnp.concatenate([basis_ref[...], zero], axis=0))
    residual_ref[...] = (samples_ref[...].astype(F32) - predicted).astype(BF16)
    update = mm(both, jnp.concatenate([zero, eval_ref[...]], axis=0))
    stepped = model_ref[...].astype(F32) + update
    limit = limit_ref[...]
    boxes = limit.shape[0]
    for i in range(0, stepped.shape[0], boxes):
        part = stepped[i : i + boxes]
        next_ref[i : i + boxes] = part - jnp.minimum(jnp.maximum(part, -limit), limit)


def finish(own, far, model, samples, limit, evals, basis_t):
    rows, width = model.shape
    k2 = own.shape[1]
    boxes = limit.shape[0]
    block = boxes
    wide = pl.BlockSpec((block, width), lambda i: (i, 0))
    slim = pl.BlockSpec((block, k2), lambda i: (i, 0))
    whole = pl.BlockSpec(evals.shape, lambda i: (0, 0))
    return pl.pallas_call(
        finish_kernel,
        grid=(rows // block,),
        in_specs=[slim, slim, wide, wide, pl.BlockSpec(limit.shape, lambda i: (0, 0)), whole, whole],
        out_specs=[wide, wide],
        out_shape=[
            jax.ShapeDtypeStruct((rows, width), F32),
            jax.ShapeDtypeStruct((rows, width), BF16),
        ],
        cost_estimate=pl.CostEstimate(
            flops=4 * rows * width * k2, bytes_accessed=10 * rows * width, transcendentals=0
        ),
        name="finish",
    )(own, far, model, samples, limit, evals, basis_t)


def on_device(mesh_shape, samples, model_prev, threshold, support, sample_basis, eval_basis, transfer_x, transfer_y):
    n_gx, n_gy = mesh_shape["gx"], mesh_shape["gy"]
    near = n_gx // 2
    gathers, lx, ly, width = model_prev.shape
    boxes = lx * ly
    rows = gathers * boxes
    basis_t = sample_basis.T
    model = model_prev.reshape(rows, width)
    data = samples.reshape(rows, width)

    coeffs = coefficients(model, data, eval_basis, basis_t)
    tables = make_tables(n_gy, near, transfer_x, transfer_y, basis_t)
    limit = threshold_map(
        support.reshape(boxes, support.shape[2]), threshold.reshape(boxes, 1), width
    )
    axes = ("gx", "gy")
    parts = {}
    for my in range(n_gy):
        for mx in range(0, near, 2):
            parts[my, mx] = swap(coeffs, axes, mesh_shape, (mx, my)) if mx or my else coeffs
    for my in range(n_gy):
        for mx in range(0, near, 2):
            parts[my, mx + 1] = swap(parts[my, mx], axes, mesh_shape, (1, 0))
    ordered = [parts[my, mx] for my in range(n_gy) for mx in range(near)]
    far, own = mix(ordered, tables)
    far = swap(far, axes, mesh_shape, (near, 0))
    model_next, residual = finish(own, far, model, data, limit, eval_basis, basis_t)
    return model_next.reshape(model_prev.shape), residual.reshape(samples.shape)


def solution(mesh):
    return jax.shard_map(
        functools.partial(on_device, dict(mesh.shape)),
        mesh=mesh,
        in_specs=(
            P("ga", "gx", "gy", None),
            P("ga", "gx", "gy", None),
            P("gx", "gy"),
            P("gx", "gy", None),
            P(),
            P(),
            P(),
            P(),
        ),
        out_specs=(P("ga", "gx", "gy", None), P("ga", "gx", "gy", None)),
        check_vma=False,
    )
```

```python
import functools

import jax
import jax.numpy as jnp
from jax import lax
from jax.experimental import pallas as pl
from jax.experimental.pallas import tpu as pltpu
from jax.sharding import PartitionSpec as P


CHUNKS = 2
PIECES = 2
F32 = jnp.float32
BF16 = jnp.bfloat16


def mm(a, b):
    return lax.dot_general(a, b, (((1,), (0,)), ((), ())), preferred_element_type=F32)


def mm_nt(a, b):
    return lax.dot_general(a, b, (((1,), (1,)), ((), ())), preferred_element_type=F32)


def swap(x, axes, mesh_shape, masks):
    sizes = [mesh_shape[axis] for axis in axes]
    total = 1
    for size in sizes:
        total *= size
    pairs = []
    for source in range(total):
        rest, coords = source, []
        for size in reversed(sizes):
            coords.append(rest % size)
            rest //= size
        coords.reverse()
        target = 0
        for coord, mask, size in zip(coords, masks, sizes):
            target = target * size + (coord ^ mask)
        pairs.append((source, target))
    return lax.ppermute(x, axes, pairs)


VMEM = pl.BlockSpec(memory_space=pltpu.VMEM)
ANY = pl.BlockSpec(memory_space=pl.ANY)
PARAMS = pltpu.CompilerParams(vmem_limit_bytes=8 << 20)


def coeff_kernel(*refs):
    model_hbm, samples_hbm, eval_hbm, basis_hbm = refs[:4]
    outs = refs[4:-4]
    model_ref, samples_ref, weight_ref, sems = refs[-4:]
    k = eval_hbm.shape[0]
    pieces, step = model_ref.shape[:2]
    copies = [
        pltpu.make_async_copy(eval_hbm, weight_ref.at[pl.ds(0, k)], sems.at[0]),
        pltpu.make_async_copy(basis_hbm, weight_ref.at[pl.ds(k, k)], sems.at[1]),
    ]
    for i in range(pieces):
        part = pl.ds(i * step, step)
        copies.append(pltpu.make_async_copy(model_hbm.at[part], model_ref.at[i], sems.at[2 + 2 * i]))
        copies.append(pltpu.make_async_copy(samples_hbm.at[part], samples_ref.at[i], sems.at[3 + 2 * i]))
    for copy in copies:
        copy.start()
    copies[0].wait()
    copies[1].wait()
    weights = weight_ref[...].T
    lane = lax.broadcasted_iota(jnp.int32, (step, 2 * k), 1)
    for i in range(pieces):
        copies[2 + 2 * i].wait()
        copies[3 + 2 * i].wait()
        top = mm(model_ref[i], weights)
        low = mm(samples_ref[i], weights)
        out_ref = outs[i * len(outs) // pieces]
        row = i * step % out_ref.shape[0]
        out_ref[row : row + step] = jnp.where(lane < k, top, low).astype(BF16)


def coefficients(model, samples, evals, basis_t, chunks):
    rows, width = model.shape
    k = evals.shape[0]
    pieces = chunks * PIECES if rows % (16 * chunks * PIECES) == 0 else chunks
    return pl.pallas_call(
        coeff_kernel,
        in_specs=[ANY] * 4,
        out_specs=[VMEM] * chunks,
        out_shape=[pltpu.VMEM((rows // chunks, 2 * k), BF16)] * chunks,
        scratch_shapes=[
            pltpu.VMEM((pieces, rows // pieces, width), BF16),
            pltpu.VMEM((pieces, rows // pieces, width), BF16),
            pltpu.VMEM((2 * k, width), BF16),
            pltpu.SemaphoreType.DMA((2 + 2 * pieces,)),
        ],
        cost_estimate=pl.CostEstimate(
            flops=8 * rows * width * k, bytes_accessed=4 * rows * (width + k), transcendentals=0
        ),
        name="coefficients",
    )(model, samples, evals, basis_t)


def table_kernel(n_gy, near, tx_ref, ty_ref, basis_ref, out_ref):
    k = basis_ref.shape[0]
    own_x, own_y = lax.axis_index("gx"), lax.axis_index("gy")
    targets = (own_x, own_x ^ near)
    flat = tx_ref.shape[1] * k

    def turned(s):
        return tx_ref[s].reshape(flat, k).T

    span = 4
    stacked = jnp.concatenate([basis_ref[...]] * span, axis=0)
    gram = mm_nt(stacked, stacked)
    row = lax.broadcasted_iota(jnp.int32, gram.shape, 0) // k
    col = lax.broadcasted_iota(jnp.int32, gram.shape, 1) // k
    gram = jnp.where(row == col, gram, 0.0).astype(BF16)
    turned_sources = [turned(own_x ^ m) for m in range(near)]
    to_targets = jnp.concatenate([turned_sources[0], turned(targets[1])], axis=0)
    y_turned = jnp.concatenate([ty_ref[s].reshape(n_gy * k, k).T for s in range(n_gy)], axis=0)
    step = span * k
    weighted = jnp.concatenate(
        [
            mm(to_targets[:, i : i + step], gram).astype(BF16)
            for i in range(0, to_targets.shape[1], step)
        ],
        axis=1,
    )
    sources = jnp.concatenate(turned_sources, axis=0)
    cross = mm_nt(sources, weighted).astype(BF16)
    zero = jnp.zeros((k, k), BF16)

    def pair(block):
        return jnp.concatenate(
            [jnp.concatenate([block, zero], axis=1), jnp.concatenate([zero, block], axis=1)], axis=0
        )

    inner = [mm(cross, pair(ty_ref[own_y, m])).astype(BF16) for m in range(n_gy)]
    lane = lax.broadcasted_iota(jnp.int32, (k, 2 * k), 1)
    for m in range(near):
        source = own_x ^ m
        stacked_inner = jnp.concatenate([part[m * k : (m + 1) * k] for part in inner], axis=0)
        normal = mm(y_turned, stacked_inner)
        to_rows = jnp.concatenate([tx_ref[source, t] for t in targets], axis=0)
        from_rows = jnp.concatenate([tx_ref[t, source] for t in targets], axis=0)
        for s in range(n_gy):
            forward = mm_nt(ty_ref[s, own_y].T, to_rows)
            back = mm(from_rows, jnp.concatenate([ty_ref[own_y, s]] * 2, axis=1))
            negated = normal[s * k : (s + 1) * k]
            slot = (s ^ own_y) * near + m
            first = jnp.where(lane < k, forward, -jnp.roll(negated, k, axis=1))
            second = jnp.where(lane < k, jnp.roll(forward, k, axis=1), -negated)
            out_ref[slot, :k, : 2 * k] = first.astype(BF16)
            out_ref[slot, :k, 2 * k :] = second.astype(BF16)
            for i in range(2):
                adjoint = jnp.where(lane < k, 0.0, back[i * k : (i + 1) * k])
                out_ref[slot, k:, 2 * k * i : 2 * k * (i + 1)] = adjoint.astype(BF16)


def make_tables(n_gy, near, transfer_x, transfer_y, basis_t):
    k = transfer_x.shape[3]
    return pl.pallas_call(
        functools.partial(table_kernel, n_gy, near),
        in_specs=[VMEM] * 3,
        out_specs=VMEM,
        out_shape=jax.ShapeDtypeStruct((n_gy * near, 2 * k, 4 * k), BF16),
        cost_estimate=pl.CostEstimate(
            flops=200000000, bytes_accessed=2000000, transcendentals=0
        ),
        compiler_params=PARAMS,
        name="tables",
    )(transfer_x, transfer_y, basis_t)


def mask_kernel(support_ref, threshold_ref, out_ref):
    count = out_ref.shape[1]
    picked = support_ref[...].T
    word, bit = picked >> 5, jnp.int32(1) << (picked & 31)
    words = count // 32
    index = lax.broadcasted_iota(jnp.int32, (words, picked.shape[1]), 0)
    bits = jnp.zeros(index.shape, jnp.int32)
    for j in range(picked.shape[0]):
        bits = bits | jnp.where(index == word[j : j + 1], bit[j : j + 1], 0)
    shift = lax.broadcasted_iota(jnp.int32, (32, picked.shape[1]), 0)
    flags = jnp.concatenate([(bits[w : w + 1] >> shift) & 1 for w in range(words)], axis=0)
    kept = flags.T != 0
    levels = threshold_ref[...].T
    ly = levels.shape[0]
    for i in range(levels.shape[1]):
        rows = slice(i * ly, (i + 1) * ly)
        out_ref[rows] = jnp.where(kept[rows], levels[:, i : i + 1], jnp.inf)


def threshold_map(support, threshold, width):
    boxes = support.shape[0]
    return pl.pallas_call(
        mask_kernel,
        in_specs=[VMEM] * 2,
        out_specs=VMEM,
        out_shape=jax.ShapeDtypeStruct((boxes, width), F32),
        cost_estimate=pl.CostEstimate(
            flops=boxes * width * 32, bytes_accessed=4 * boxes * width, transcendentals=0
        ),
        compiler_params=PARAMS,
        name="threshold_map",
    )(support, threshold)


def mix_kernel(count, *refs):
    tables_ref, far_ref, own_ref = refs[count:]
    k2 = refs[0].shape[1]
    tables = tables_ref[...].reshape(count * k2, 2 * k2)
    for i in range(0, refs[0].shape[0], 256):
        mixed = mm(jnp.concatenate([ref[i : i + 256] for ref in refs[:count]], axis=1), tables)
        own_ref[i : i + 256] = mixed[:, :k2]
        far_ref[i : i + 256] = mixed[:, k2:].astype(BF16)


def mix(parts, tables):
    rows, k2 = parts[0].shape
    count = len(parts)
    return pl.pallas_call(
        functools.partial(mix_kernel, count),
        in_specs=[VMEM] * (count + 1),
        out_specs=[VMEM, VMEM],
        out_shape=[
            jax.ShapeDtypeStruct((rows, k2), BF16),
            jax.ShapeDtypeStruct((rows, k2), F32),
        ],
        cost_estimate=pl.CostEstimate(
            flops=4 * rows * count * k2 * k2,
            bytes_accessed=2 * rows * k2 * count,
            transcendentals=0,
        ),
        compiler_params=PARAMS,
        name="mix",
    )(*parts, tables)


def finish_kernel(first, *refs):
    own_ref, far_ref, model_ref, samples_ref, limit_ref, eval_ref, basis_ref = refs[:7]
    next_ref, residual_ref = refs[-2:]
    zero = jnp.zeros(eval_ref.shape, BF16)
    to_data = jnp.concatenate([basis_ref[...], zero], axis=0)
    to_model = jnp.concatenate([zero, eval_ref[...]], axis=0)
    limit = limit_ref[...]
    boxes = limit.shape[0]
    start = pl.program_id(0) * next_ref.shape[0]
    for i in range(0, next_ref.shape[0], boxes):
        here = pl.multiple_of(start + i, boxes)
        rows, whole = pl.ds(here, boxes), pl.ds(first + here, boxes)
        both = (own_ref[rows] + far_ref[rows].astype(F32)).astype(BF16)
        predicted = mm(both, to_data)
        residual_ref[i : i + boxes] = (samples_ref[whole].astype(F32) - predicted).astype(BF16)
        stepped = model_ref[whole].astype(F32) + mm(both, to_model)
        next_ref[i : i + boxes] = stepped - jnp.minimum(jnp.maximum(stepped, -limit), limit)


def finish(own, far, model, samples, limit, evals, basis_t, first, earlier):
    total, width = model.shape
    rows, k2 = own.shape
    block = limit.shape[0]
    skip = first // block
    wide = pl.BlockSpec((block, width), lambda i: (i + skip, 0))
    return pl.pallas_call(
        functools.partial(finish_kernel, first),
        grid=(rows // block,),
        in_specs=[VMEM] * 7 + [ANY] * len(earlier),
        out_specs=[wide, wide],
        out_shape=[
            jax.ShapeDtypeStruct((total, width), F32),
            jax.ShapeDtypeStruct((total, width), BF16),
        ],
        input_output_aliases={7 + i: i for i in range(len(earlier))},
        cost_estimate=pl.CostEstimate(
            flops=4 * rows * width * k2, bytes_accessed=10 * rows * width, transcendentals=0
        ),
        compiler_params=PARAMS,
        name="finish",
    )(own, far, model, samples, limit, evals, basis_t, *earlier)


def on_device(mesh_shape, samples, model_prev, threshold, support, sample_basis, eval_basis, transfer_x, transfer_y):
    n_gx, n_gy = mesh_shape["gx"], mesh_shape["gy"]
    near = n_gx // 2
    gathers, lx, ly, width = model_prev.shape
    boxes = lx * ly
    rows = gathers * boxes
    basis_t = sample_basis.T
    model = model_prev.reshape(rows, width)
    data = samples.reshape(rows, width)
    chunks = CHUNKS if gathers % CHUNKS == 0 else 1
    size = rows // chunks
    axes = ("gx", "gy")

    near_parts = []
    all_coeffs = coefficients(model, data, eval_basis, basis_t, chunks)
    for coeffs in all_coeffs:
        parts = {}
        for my in reversed(range(n_gy)):
            for mx in reversed(range(0, near, 2)):
                parts[my, mx] = swap(coeffs, axes, mesh_shape, (mx, my)) if mx or my else coeffs
        near_parts.append(parts)
    tables = make_tables(n_gy, near, transfer_x, transfer_y, basis_t)
    limit = threshold_map(
        support.reshape(boxes, support.shape[2]), threshold, width
    )
    mixed = []
    for parts in near_parts:
        for my in range(n_gy):
            for mx in range(0, near, 2):
                parts[my, mx + 1] = swap(parts[my, mx], axes, mesh_shape, (1, 0))
        ordered = [parts[my, mx] for my in range(n_gy) for mx in range(near)]
        far, own = mix(ordered, tables)
        mixed.append((own, swap(far, axes, mesh_shape, (near, 0))))
    outs = ()
    for c, (own, far) in enumerate(mixed):
        outs = finish(own, far, model, data, limit, eval_basis, basis_t, c * size, outs)
    model_next, residual = outs
    return model_next.reshape(model_prev.shape), residual.reshape(samples.shape)


def step(mesh_shape, *args):
    return on_device(mesh_shape, *args)


def solution(mesh):
    return jax.shard_map(
        functools.partial(step, dict(mesh.shape)),
        mesh=mesh,
        in_specs=(
            P("ga", "gx", "gy", None),
            P("ga", "gx", "gy", None),
            P("gx", "gy"),
            P("gx", "gy", None),
            P(),
            P(),
            P(),
            P(),
        ),
        out_specs=(P("ga", "gx", "gy", None), P("ga", "gx", "gy", None)),
        check_vma=False,
    )
```

```python
import functools

import jax
import jax.numpy as jnp
from jax import lax
from jax.experimental import pallas as pl
from jax.experimental.pallas import tpu as pltpu
from jax.sharding import PartitionSpec as P


SIZES = (1, 1)
F32 = jnp.float32
BF16 = jnp.bfloat16


def mm(a, b):
    return lax.dot_general(a, b, (((1,), (0,)), ((), ())), preferred_element_type=F32)


def mm_nt(a, b):
    return lax.dot_general(a, b, (((1,), (1,)), ((), ())), preferred_element_type=F32)


def swap(x, axes, mesh_shape, masks):
    sizes = [mesh_shape[axis] for axis in axes]
    total = 1
    for size in sizes:
        total *= size
    pairs = []
    for source in range(total):
        rest, coords = source, []
        for size in reversed(sizes):
            coords.append(rest % size)
            rest //= size
        coords.reverse()
        target = 0
        for coord, mask, size in zip(coords, masks, sizes):
            target = target * size + (coord ^ mask)
        pairs.append((source, target))
    return lax.ppermute(x, axes, pairs)


VMEM = pl.BlockSpec(memory_space=pltpu.VMEM)
ANY = pl.BlockSpec(memory_space=pl.ANY)
PARAMS = pltpu.CompilerParams(vmem_limit_bytes=8 << 20)


def split(gathers):
    parts = sum(SIZES)
    return [gathers * part // parts for part in SIZES] if gathers % parts == 0 else [gathers]


def coeff_kernel(count, *refs):
    model_hbm, samples_hbm, eval_hbm, basis_hbm = refs[:4]
    outs = refs[4 : 4 + count]
    model_ref, samples_ref, weight_ref, sems = refs[4 + count :]
    k = eval_hbm.shape[0]
    copies = [
        pltpu.make_async_copy(eval_hbm, weight_ref.at[pl.ds(0, k)], sems.at[0]),
        pltpu.make_async_copy(basis_hbm, weight_ref.at[pl.ds(k, k)], sems.at[1]),
    ]
    first = 0
    for i, out_ref in enumerate(outs):
        part = pl.ds(first, out_ref.shape[0])
        first += out_ref.shape[0]
        copies.append(pltpu.make_async_copy(model_hbm.at[part], model_ref.at[part], sems.at[2 + 2 * i]))
        copies.append(pltpu.make_async_copy(samples_hbm.at[part], samples_ref.at[part], sems.at[3 + 2 * i]))
    for copy in copies:
        copy.start()
    copies[0].wait()
    copies[1].wait()
    weights = weight_ref[...].T
    first = 0
    for i, out_ref in enumerate(outs):
        rows = out_ref.shape[0]
        part = pl.ds(first, rows)
        first += rows
        copies[2 + 2 * i].wait()
        copies[3 + 2 * i].wait()
        top = mm(model_ref[part], weights)
        low = mm(samples_ref[part], weights)
        lane = lax.broadcasted_iota(jnp.int32, (rows, 2 * k), 1)
        out_ref[...] = jnp.where(lane < k, top, low).astype(BF16)


def coefficients(model, samples, evals, basis_t, counts):
    rows, width = model.shape
    k = evals.shape[0]
    return pl.pallas_call(
        functools.partial(coeff_kernel, len(counts)),
        in_specs=[ANY] * 4,
        out_specs=[VMEM] * len(counts),
        out_shape=[pltpu.VMEM((count, 2 * k), BF16) for count in counts],
        scratch_shapes=[
            pltpu.VMEM((rows, width), BF16),
            pltpu.VMEM((rows, width), BF16),
            pltpu.VMEM((2 * k, width), BF16),
            pltpu.SemaphoreType.DMA((2 + 2 * len(counts),)),
        ],
        cost_estimate=pl.CostEstimate(
            flops=8 * rows * width * k, bytes_accessed=4 * rows * (width + k), transcendentals=0
        ),
        name="coefficients",
    )(model, samples, evals, basis_t)


def diagonal(block, count):
    zero = jnp.zeros_like(block)
    rows = [jnp.concatenate([block if i == j else zero for j in range(count)], axis=1) for i in range(count)]
    return jnp.concatenate(rows, axis=0)


def table_kernel(n_gy, near, tx_ref, ty_ref, basis_ref, gather_ref, scatter_ref):
    k = basis_ref.shape[0]
    own_x, own_y = lax.axis_index("gx"), lax.axis_index("gy")
    flat = tx_ref.shape[1] * k
    masks = sorted({*range(near), near, near + 1})
    turned = {m: tx_ref[own_x ^ m].reshape(flat, k).T for m in masks}
    span = 4
    stacked = jnp.concatenate([basis_ref[...]] * span, axis=0)
    gram = mm_nt(stacked, stacked)
    row = lax.broadcasted_iota(jnp.int32, gram.shape, 0) // k
    col = lax.broadcasted_iota(jnp.int32, gram.shape, 1) // k
    gram = jnp.where(row == col, gram, 0.0).astype(BF16)
    lane = lax.broadcasted_iota(jnp.int32, (k, 2 * k), 1)

    def crossed(sources, targets):
        ends = jnp.concatenate([turned[m] for m in targets], axis=0)
        step = span * k
        ends = jnp.concatenate(
            [mm(ends[:, i : i + step], gram).astype(BF16) for i in range(0, flat, step)], axis=1
        )
        return mm_nt(jnp.concatenate([turned[m] for m in sources], axis=0), ends).astype(BF16)

    def store(out_ref, slot, where, i, forward, normal, back):
        here = slice(i // 2 * 2 * k, i // 2 * 2 * k + 2 * k)
        forward, normal = forward[:, here], normal[:, here]
        if i % 2:
            forward = jnp.roll(forward, k, axis=1)
        else:
            normal = jnp.roll(normal, k, axis=1)
        lanes = slice(where * 2 * k, (where + 1) * 2 * k)
        out_ref[slot, :k, lanes] = jnp.where(lane < k, forward, -normal).astype(BF16)
        out_ref[slot, k:, lanes] = jnp.where(lane < k, 0.0, back).astype(BF16)

    targets = (0, near)
    cross = crossed(range(near), targets)
    y_turned = [ty_ref[s].reshape(n_gy * k, k).T for s in range(n_gy)]
    inner = [mm(cross, diagonal(ty_ref[own_y, m], 2)).astype(BF16) for m in range(n_gy)]
    for m in range(near):
        source = own_x ^ m
        parts = jnp.concatenate([part[m * k : (m + 1) * k] for part in inner], axis=0)
        to_rows = jnp.concatenate([tx_ref[source, own_x ^ t] for t in targets], axis=0)
        from_rows = jnp.concatenate([tx_ref[own_x ^ t, source] for t in targets], axis=0)
        for s in range(n_gy):
            normal = mm(y_turned[s], parts)
            forward = mm_nt(ty_ref[s, own_y].T, to_rows)
            back = mm(from_rows, jnp.concatenate([ty_ref[own_y, s]] * 2, axis=1))
            for i in range(2):
                store(gather_ref, (s ^ own_y) * near + m, i, i, forward, normal, back[i * k : (i + 1) * k])

    sources = (0, 1, near, near + 1)
    targets = range(0, near, 2)
    count = len(targets)
    cross = crossed(sources, targets)
    own_turned = ty_ref[own_y].reshape(n_gy * k, k).T
    for my in range(n_gy):
        target_y = own_y ^ my
        inner = [mm(cross, diagonal(ty_ref[target_y, m], count)).astype(BF16) for m in range(n_gy)]
        y_forward = ty_ref[own_y, target_y].T
        y_back = jnp.concatenate([ty_ref[target_y, own_y]] * 2, axis=1)
        for n, m in enumerate(sources):
            source = own_x ^ m
            parts = jnp.concatenate([part[n * k : (n + 1) * k] for part in inner], axis=0)
            normal = mm(own_turned, parts)
            forward = mm_nt(y_forward, jnp.concatenate([tx_ref[source, own_x ^ t] for t in targets], axis=0))
            back = mm(jnp.concatenate([tx_ref[own_x ^ t, source] for t in targets], axis=0), y_back)
            for i in range(count):
                store(scatter_ref, n, my * count + i, i, forward, normal, back[i * k : (i + 1) * k])


def make_tables(n_gy, near, transfer_x, transfer_y, basis_t):
    k = transfer_x.shape[3]
    return pl.pallas_call(
        functools.partial(table_kernel, n_gy, near),
        in_specs=[VMEM] * 3,
        out_specs=[VMEM] * 2,
        out_shape=[
            jax.ShapeDtypeStruct((n_gy * near, 2 * k, 4 * k), BF16),
            jax.ShapeDtypeStruct((4, 2 * k, n_gy * near * k), BF16),
        ],
        cost_estimate=pl.CostEstimate(
            flops=200000000, bytes_accessed=2000000, transcendentals=0
        ),
        compiler_params=PARAMS,
        name="tables",
    )(transfer_x, transfer_y, basis_t)


def mask_kernel(support_ref, threshold_ref, out_ref):
    count = out_ref.shape[1]
    picked = support_ref[...].T
    word, bit = picked >> 5, jnp.int32(1) << (picked & 31)
    words = count // 32
    index = lax.broadcasted_iota(jnp.int32, (words, picked.shape[1]), 0)
    bits = jnp.zeros(index.shape, jnp.int32)
    for j in range(picked.shape[0]):
        bits = bits | jnp.where(index == word[j : j + 1], bit[j : j + 1], 0)
    shift = lax.broadcasted_iota(jnp.int32, (32, picked.shape[1]), 0)
    flags = jnp.concatenate([(bits[w : w + 1] >> shift) & 1 for w in range(words)], axis=0)
    kept = flags.T != 0
    levels = threshold_ref[...].T
    ly = levels.shape[0]
    for i in range(levels.shape[1]):
        rows = slice(i * ly, (i + 1) * ly)
        out_ref[rows] = jnp.where(kept[rows], levels[:, i : i + 1], jnp.inf)


def threshold_map(support, threshold, width):
    boxes = support.shape[0]
    return pl.pallas_call(
        mask_kernel,
        in_specs=[VMEM] * 2,
        out_specs=VMEM,
        out_shape=jax.ShapeDtypeStruct((boxes, width), F32),
        cost_estimate=pl.CostEstimate(
            flops=boxes * width * 32, bytes_accessed=4 * boxes * width, transcendentals=0
        ),
        compiler_params=PARAMS,
        name="threshold_map",
    )(support, threshold)


def mix_kernel(count, *refs):
    tables_ref, own_ref = refs[count : count + 2]
    sent = refs[count + 2 :]
    k2 = refs[0].shape[1]
    rows = refs[0].shape[0]
    tables = tables_ref[...].reshape(count * k2, tables_ref.shape[2])
    for i in range(0, rows, 256):
        here = slice(i, min(i + 256, rows))
        mixed = mm(jnp.concatenate([ref[here] for ref in refs[:count]], axis=1), tables)
        own_ref[here] = mixed[:, :k2]
        for j, out_ref in enumerate(sent):
            out_ref[here] = mixed[:, (j + 1) * k2 : (j + 2) * k2].astype(BF16)


def mix(parts, tables):
    rows, k2 = parts[0].shape
    count = len(parts)
    others = tables.shape[2] // k2 - 1
    return pl.pallas_call(
        functools.partial(mix_kernel, count),
        in_specs=[VMEM] * (count + 1),
        out_specs=[VMEM] * (1 + others),
        out_shape=[pltpu.VMEM((rows, k2), F32)] + [pltpu.VMEM((rows, k2), BF16)] * others,
        cost_estimate=pl.CostEstimate(
            flops=2 * rows * count * k2 * tables.shape[2],
            bytes_accessed=2 * rows * k2 * (count + others),
            transcendentals=0,
        ),
        compiler_params=PARAMS,
        name="mix",
    )(*parts, tables)


def finish_kernel(first, count, *refs):
    own_ref, arrived = refs[0], refs[1 : 1 + count]
    model_ref, samples_ref, limit_ref, eval_ref, basis_ref = refs[1 + count : 6 + count]
    next_hbm, residual_hbm, next_ref, residual_ref, sems = refs[-5:]
    zero = jnp.zeros(eval_ref.shape, BF16)
    to_data = jnp.concatenate([basis_ref[...], zero], axis=0)
    to_model = jnp.concatenate([zero, eval_ref[...]], axis=0)
    limit = limit_ref[...]
    boxes = limit.shape[0]
    copies = []
    for i in range(next_ref.shape[0]):
        rows, whole = pl.ds(i * boxes, boxes), pl.ds(first + i * boxes, boxes)
        both = own_ref[rows]
        for ref in arrived:
            both = both + ref[rows].astype(F32)
        both = both.astype(BF16)
        predicted = mm(both, to_data)
        residual_ref[i] = (samples_ref[whole].astype(F32) - predicted).astype(BF16)
        copies.append(pltpu.make_async_copy(residual_ref.at[i], residual_hbm.at[whole], sems.at[2 * i]))
        copies[-1].start()
        stepped = model_ref[whole].astype(F32) + mm(both, to_model)
        next_ref[i] = stepped - jnp.minimum(jnp.maximum(stepped, -limit), limit)
        copies.append(pltpu.make_async_copy(next_ref.at[i], next_hbm.at[whole], sems.at[2 * i + 1]))
        copies[-1].start()
    for copy in copies:
        copy.wait()


def finish(own, arrived, model, samples, limit, evals, basis_t, first, earlier):
    total, width = model.shape
    rows, k2 = own.shape
    boxes = limit.shape[0]
    pieces = rows // boxes
    return pl.pallas_call(
        functools.partial(finish_kernel, first, len(arrived)),
        in_specs=[VMEM] * (6 + len(arrived)) + [ANY] * len(earlier),
        out_specs=[ANY, ANY],
        out_shape=[
            jax.ShapeDtypeStruct((total, width), F32),
            jax.ShapeDtypeStruct((total, width), BF16),
        ],
        scratch_shapes=[
            pltpu.VMEM((pieces, boxes, width), F32),
            pltpu.VMEM((pieces, boxes, width), BF16),
            pltpu.SemaphoreType.DMA((2 * pieces,)),
        ],
        input_output_aliases={6 + len(arrived) + i: i for i in range(len(earlier))},
        cost_estimate=pl.CostEstimate(
            flops=4 * rows * width * k2, bytes_accessed=10 * rows * width, transcendentals=0
        ),
        compiler_params=PARAMS,
        name="finish",
    )(own, *arrived, model, samples, limit, evals, basis_t, *earlier)


def on_device(mesh_shape, samples, model_prev, threshold, support, sample_basis, eval_basis, transfer_x, transfer_y):
    n_gx, n_gy = mesh_shape["gx"], mesh_shape["gy"]
    near = n_gx // 2
    gathers, lx, ly, width = model_prev.shape
    boxes = lx * ly
    rows = gathers * boxes
    basis_t = sample_basis.T
    model = model_prev.reshape(rows, width)
    data = samples.reshape(rows, width)
    counts = [count * boxes for count in split(gathers)]
    firsts = [sum(counts[:c]) for c in range(len(counts))]
    axes = ("gx", "gy")

    def exchange(x, mx, my):
        return swap(x, axes, mesh_shape, (mx, my))

    around = [(mx, my) for my in range(n_gy) for mx in range(0, near, 2)]
    first, second = coefficients(model, data, eval_basis, basis_t, counts)
    gather, scatter = make_tables(n_gy, near, transfer_x, transfer_y, basis_t)
    limit = threshold_map(
        support.reshape(boxes, support.shape[2]), threshold, width
    )

    parts = []
    for mx, my in around:
        part = exchange(first, mx, my) if mx or my else first
        parts += [part, exchange(part, 1, 0)]
    own_first, far = mix(parts, gather)
    far_first = exchange(far, near, 0)

    far = exchange(second, near, 0)
    parts = [second, exchange(second, 1, 0), far, exchange(far, 1, 0)]
    own_second, *sent = mix(parts, scatter)
    arrived = [exchange(x, mx, my) for x, (mx, my) in zip(sent, around[1:])]

    outs = ()
    outs = finish(own_second, arrived, model, data, limit, eval_basis, basis_t, firsts[1], outs)
    outs = finish(own_first, [far_first], model, data, limit, eval_basis, basis_t, firsts[0], outs)
    model_next, residual = outs
    return model_next.reshape(model_prev.shape), residual.reshape(samples.shape)


def step(mesh_shape, *args):
    return on_device(mesh_shape, *args)


def solution(mesh):
    return jax.shard_map(
        functools.partial(step, dict(mesh.shape)),
        mesh=mesh,
        in_specs=(
            P("ga", "gx", "gy", None),
            P("ga", "gx", "gy", None),
            P("gx", "gy"),
            P("gx", "gy", None),
            P(),
            P(),
            P(),
            P(),
        ),
        out_specs=(P("ga", "gx", "gy", None), P("ga", "gx", "gy", None)),
        check_vma=False,
    )
```

```python
import functools

import jax
import jax.numpy as jnp
from jax import lax
from jax.experimental import pallas as pl
from jax.experimental.pallas import tpu as pltpu
from jax.sharding import PartitionSpec as P


SIZES = (1, 1)
CUTS = (0, 1)
F32 = jnp.float32
BF16 = jnp.bfloat16


def mm(a, b):
    return lax.dot_general(a, b, (((1,), (0,)), ((), ())), preferred_element_type=F32)


def mm_nt(a, b):
    return lax.dot_general(a, b, (((1,), (1,)), ((), ())), preferred_element_type=F32)


def swap(x, axes, mesh_shape, masks):
    sizes = [mesh_shape[axis] for axis in axes]
    total = 1
    for size in sizes:
        total *= size
    pairs = []
    for source in range(total):
        rest, coords = source, []
        for size in reversed(sizes):
            coords.append(rest % size)
            rest //= size
        coords.reverse()
        target = 0
        for coord, mask, size in zip(coords, masks, sizes):
            target = target * size + (coord ^ mask)
        pairs.append((source, target))
    return lax.ppermute(x, axes, pairs)


VMEM = pl.BlockSpec(memory_space=pltpu.VMEM)
ANY = pl.BlockSpec(memory_space=pl.ANY)
PARAMS = pltpu.CompilerParams(vmem_limit_bytes=8 << 20)


def split(gathers):
    parts = sum(SIZES)
    return [gathers * part // parts for part in SIZES] if gathers % parts == 0 else [gathers]


def coeff_kernel(count, *refs):
    model_hbm, samples_hbm, eval_hbm, basis_hbm = refs[:4]
    outs = refs[4 : 4 + count]
    model_ref, samples_ref, weight_ref, sems = refs[4 + count :]
    k = eval_hbm.shape[0]
    copies = [
        pltpu.make_async_copy(eval_hbm, weight_ref.at[pl.ds(0, k)], sems.at[0]),
        pltpu.make_async_copy(basis_hbm, weight_ref.at[pl.ds(k, k)], sems.at[1]),
    ]
    first = 0
    for i, out_ref in enumerate(outs):
        part = pl.ds(first, out_ref.shape[0])
        first += out_ref.shape[0]
        copies.append(pltpu.make_async_copy(model_hbm.at[part], model_ref.at[part], sems.at[2 + 2 * i]))
        copies.append(pltpu.make_async_copy(samples_hbm.at[part], samples_ref.at[part], sems.at[3 + 2 * i]))
    for copy in copies:
        copy.start()
    copies[0].wait()
    copies[1].wait()
    weights = weight_ref[...].T
    first = 0
    for i, out_ref in enumerate(outs):
        rows = out_ref.shape[0]
        part = pl.ds(first, rows)
        first += rows
        copies[2 + 2 * i].wait()
        copies[3 + 2 * i].wait()
        top = mm(model_ref[part], weights)
        low = mm(samples_ref[part], weights)
        lane = lax.broadcasted_iota(jnp.int32, (rows, 2 * k), 1)
        out_ref[...] = jnp.where(lane < k, top, low).astype(BF16)


def coefficients(model, samples, evals, basis_t, counts):
    rows, width = model.shape
    k = evals.shape[0]
    return pl.pallas_call(
        functools.partial(coeff_kernel, len(counts)),
        in_specs=[ANY] * 4,
        out_specs=[VMEM] * len(counts),
        out_shape=[pltpu.VMEM((count, 2 * k), BF16) for count in counts],
        scratch_shapes=[
            pltpu.VMEM((rows, width), BF16),
            pltpu.VMEM((rows, width), BF16),
            pltpu.VMEM((2 * k, width), BF16),
            pltpu.SemaphoreType.DMA((2 + 2 * len(counts),)),
        ],
        cost_estimate=pl.CostEstimate(
            flops=8 * rows * width * k, bytes_accessed=4 * rows * (width + k), transcendentals=0
        ),
        name="coefficients",
    )(model, samples, evals, basis_t)


def diagonal(block, count):
    zero = jnp.zeros_like(block)
    rows = [jnp.concatenate([block if i == j else zero for j in range(count)], axis=1) for i in range(count)]
    return jnp.concatenate(rows, axis=0)


def table_kernel(n_gy, near, tx_ref, ty_ref, basis_ref, gather_ref, scatter_ref):
    k = basis_ref.shape[0]
    own_x, own_y = lax.axis_index("gx"), lax.axis_index("gy")
    flat = tx_ref.shape[1] * k
    masks = sorted({*range(near), near, near + 1})
    turned = {m: tx_ref[own_x ^ m].reshape(flat, k).T for m in masks}
    span = 4
    stacked = jnp.concatenate([basis_ref[...]] * span, axis=0)
    gram = mm_nt(stacked, stacked)
    row = lax.broadcasted_iota(jnp.int32, gram.shape, 0) // k
    col = lax.broadcasted_iota(jnp.int32, gram.shape, 1) // k
    gram = jnp.where(row == col, gram, 0.0).astype(BF16)
    lane = lax.broadcasted_iota(jnp.int32, (k, 2 * k), 1)

    def crossed(sources, targets):
        ends = jnp.concatenate([turned[m] for m in targets], axis=0)
        step = span * k
        ends = jnp.concatenate(
            [mm(ends[:, i : i + step], gram).astype(BF16) for i in range(0, flat, step)], axis=1
        )
        return mm_nt(jnp.concatenate([turned[m] for m in sources], axis=0), ends).astype(BF16)

    def store(out_ref, slot, where, i, forward, normal, back):
        here = slice(i // 2 * 2 * k, i // 2 * 2 * k + 2 * k)
        forward, normal = forward[:, here], normal[:, here]
        if i % 2:
            forward = jnp.roll(forward, k, axis=1)
        else:
            normal = jnp.roll(normal, k, axis=1)
        lanes = slice(where * 2 * k, (where + 1) * 2 * k)
        out_ref[slot, :k, lanes] = jnp.where(lane < k, forward, -normal).astype(BF16)
        out_ref[slot, k:, lanes] = jnp.where(lane < k, 0.0, back).astype(BF16)

    targets = (0, near)
    cross = crossed(range(near), targets)
    y_turned = [ty_ref[s].reshape(n_gy * k, k).T for s in range(n_gy)]
    inner = [mm(cross, diagonal(ty_ref[own_y, m], 2)).astype(BF16) for m in range(n_gy)]
    for m in range(near):
        source = own_x ^ m
        parts = jnp.concatenate([part[m * k : (m + 1) * k] for part in inner], axis=0)
        to_rows = jnp.concatenate([tx_ref[source, own_x ^ t] for t in targets], axis=0)
        from_rows = jnp.concatenate([tx_ref[own_x ^ t, source] for t in targets], axis=0)
        for s in range(n_gy):
            normal = mm(y_turned[s], parts)
            forward = mm_nt(ty_ref[s, own_y].T, to_rows)
            back = mm(from_rows, jnp.concatenate([ty_ref[own_y, s]] * 2, axis=1))
            for i in range(2):
                store(gather_ref, (s ^ own_y) * near + m, i, i, forward, normal, back[i * k : (i + 1) * k])

    sources = (0, 1, near, near + 1)
    targets = range(0, near, 2)
    count = len(targets)
    cross = crossed(sources, targets)
    own_turned = ty_ref[own_y].reshape(n_gy * k, k).T
    for my in range(n_gy):
        target_y = own_y ^ my
        inner = [mm(cross, diagonal(ty_ref[target_y, m], count)).astype(BF16) for m in range(n_gy)]
        y_forward = ty_ref[own_y, target_y].T
        y_back = jnp.concatenate([ty_ref[target_y, own_y]] * 2, axis=1)
        for n, m in enumerate(sources):
            source = own_x ^ m
            parts = jnp.concatenate([part[n * k : (n + 1) * k] for part in inner], axis=0)
            normal = mm(own_turned, parts)
            forward = mm_nt(y_forward, jnp.concatenate([tx_ref[source, own_x ^ t] for t in targets], axis=0))
            back = mm(jnp.concatenate([tx_ref[own_x ^ t, source] for t in targets], axis=0), y_back)
            for i in range(count):
                store(scatter_ref, n, my * count + i, i, forward, normal, back[i * k : (i + 1) * k])


def make_tables(n_gy, near, transfer_x, transfer_y, basis_t):
    k = transfer_x.shape[3]
    return pl.pallas_call(
        functools.partial(table_kernel, n_gy, near),
        in_specs=[VMEM] * 3,
        out_specs=[VMEM] * 2,
        out_shape=[
            jax.ShapeDtypeStruct((n_gy * near, 2 * k, 4 * k), BF16),
            jax.ShapeDtypeStruct((4, 2 * k, n_gy * near * k), BF16),
        ],
        cost_estimate=pl.CostEstimate(
            flops=200000000, bytes_accessed=2000000, transcendentals=0
        ),
        compiler_params=PARAMS,
        name="tables",
    )(transfer_x, transfer_y, basis_t)


def mask_kernel(support_ref, threshold_ref, out_ref):
    count = out_ref.shape[1]
    picked = support_ref[...].T
    word, bit = picked >> 5, jnp.int32(1) << (picked & 31)
    words = count // 32
    index = lax.broadcasted_iota(jnp.int32, (words, picked.shape[1]), 0)
    bits = jnp.zeros(index.shape, jnp.int32)
    for j in range(picked.shape[0]):
        bits = bits | jnp.where(index == word[j : j + 1], bit[j : j + 1], 0)
    shift = lax.broadcasted_iota(jnp.int32, (32, picked.shape[1]), 0)
    flags = jnp.concatenate([(bits[w : w + 1] >> shift) & 1 for w in range(words)], axis=0)
    kept = flags.T != 0
    levels = threshold_ref[...].T
    ly = levels.shape[0]
    for i in range(levels.shape[1]):
        rows = slice(i * ly, (i + 1) * ly)
        out_ref[rows] = jnp.where(kept[rows], levels[:, i : i + 1], jnp.inf)


def threshold_map(support, threshold, width):
    boxes = support.shape[0]
    return pl.pallas_call(
        mask_kernel,
        in_specs=[VMEM] * 2,
        out_specs=VMEM,
        out_shape=jax.ShapeDtypeStruct((boxes, width), F32),
        cost_estimate=pl.CostEstimate(
            flops=boxes * width * 32, bytes_accessed=4 * boxes * width, transcendentals=0
        ),
        compiler_params=PARAMS,
        name="threshold_map",
    )(support, threshold)


def head_kernel(count, *refs):
    tables_ref, sum_ref = refs[count:]
    k2 = refs[0].shape[1]
    tables = tables_ref[:count].reshape(count * k2, tables_ref.shape[2])
    sum_ref[...] = mm(jnp.concatenate([ref[...] for ref in refs[:count]], axis=1), tables)


def tail_kernel(cuts, sum_ref, part_ref, tables_ref, own_ref, *sent):
    rows, k2 = part_ref.shape
    size = rows // cuts
    table = tables_ref[tables_ref.shape[0] - 1]
    for i in range(0, rows, size):
        here = slice(i, i + size)
        mixed = sum_ref[here] + mm(part_ref[here], table)
        own_ref[here] = mixed[:, :k2]
        for j in range(table.shape[1] // k2 - 1):
            sent[j * cuts + i // size][...] = mixed[:, (j + 1) * k2 : (j + 2) * k2].astype(BF16)


def mix_head(parts, tables):
    rows, k2 = parts[0].shape
    count, width = len(parts), tables.shape[2]
    return pl.pallas_call(
        functools.partial(head_kernel, count),
        in_specs=[VMEM] * (count + 1),
        out_specs=VMEM,
        out_shape=pltpu.VMEM((rows, width), F32),
        cost_estimate=pl.CostEstimate(
            flops=2 * rows * count * k2 * width,
            bytes_accessed=2 * rows * (k2 * count + 2 * width),
            transcendentals=0,
        ),
        compiler_params=PARAMS,
        name="mix_head",
    )(*parts, tables)


def mix_tail(sums, part, tables, cuts=1):
    rows, k2 = part.shape
    others = tables.shape[2] // k2 - 1
    return pl.pallas_call(
        functools.partial(tail_kernel, cuts),
        in_specs=[VMEM] * 3,
        out_specs=[VMEM] * (1 + others * cuts),
        out_shape=[pltpu.VMEM((rows, k2), F32)]
        + [pltpu.VMEM((rows // cuts, k2), BF16)] * (others * cuts),
        cost_estimate=pl.CostEstimate(
            flops=2 * rows * k2 * tables.shape[2],
            bytes_accessed=2 * rows * (k2 + 2 * tables.shape[2]),
            transcendentals=0,
        ),
        compiler_params=PARAMS,
        name="mix_tail",
    )(sums, part, tables)


def finish_kernel(first, skip, count, *refs):
    own_ref, arrived = refs[0], refs[1 : 1 + count]
    model_ref, samples_ref, limit_ref, eval_ref, basis_ref = refs[1 + count : 6 + count]
    next_hbm, residual_hbm, next_ref, residual_ref, sems = refs[-5:]
    zero = jnp.zeros(eval_ref.shape, BF16)
    to_data = jnp.concatenate([basis_ref[...], zero], axis=0)
    to_model = jnp.concatenate([zero, eval_ref[...]], axis=0)
    limit = limit_ref[...]
    boxes = limit.shape[0]
    copies = []
    for i in range(next_ref.shape[0]):
        rows, whole = pl.ds(i * boxes, boxes), pl.ds(first + skip + i * boxes, boxes)
        both = own_ref[pl.ds(skip + i * boxes, boxes)]
        for ref in arrived:
            both = both + ref[rows].astype(F32)
        both = both.astype(BF16)
        predicted = mm(both, to_data)
        residual_ref[i] = (samples_ref[whole].astype(F32) - predicted).astype(BF16)
        copies.append(pltpu.make_async_copy(residual_ref.at[i], residual_hbm.at[whole], sems.at[2 * i]))
        copies[-1].start()
        stepped = model_ref[whole].astype(F32) + mm(both, to_model)
        next_ref[i] = stepped - jnp.minimum(jnp.maximum(stepped, -limit), limit)
        copies.append(pltpu.make_async_copy(next_ref.at[i], next_hbm.at[whole], sems.at[2 * i + 1]))
        copies[-1].start()
    for copy in copies:
        copy.wait()


def finish(own, arrived, model, samples, limit, evals, basis_t, first, skip, earlier):
    total, width = model.shape
    rows, k2 = arrived[0].shape
    boxes = limit.shape[0]
    pieces = rows // boxes
    return pl.pallas_call(
        functools.partial(finish_kernel, first, skip, len(arrived)),
        in_specs=[VMEM] * (6 + len(arrived)) + [ANY] * len(earlier),
        out_specs=[ANY, ANY],
        out_shape=[
            jax.ShapeDtypeStruct((total, width), F32),
            jax.ShapeDtypeStruct((total, width), BF16),
        ],
        scratch_shapes=[
            pltpu.VMEM((pieces, boxes, width), F32),
            pltpu.VMEM((pieces, boxes, width), BF16),
            pltpu.SemaphoreType.DMA((2 * pieces,)),
        ],
        input_output_aliases={6 + len(arrived) + i: i for i in range(len(earlier))},
        cost_estimate=pl.CostEstimate(
            flops=4 * rows * width * k2, bytes_accessed=10 * rows * width, transcendentals=0
        ),
        compiler_params=PARAMS,
        name="finish",
    )(own, *arrived, model, samples, limit, evals, basis_t, *earlier)


def on_device(mesh_shape, samples, model_prev, threshold, support, sample_basis, eval_basis, transfer_x, transfer_y):
    n_gx, n_gy = mesh_shape["gx"], mesh_shape["gy"]
    near = n_gx // 2
    gathers, lx, ly, width = model_prev.shape
    boxes = lx * ly
    rows = gathers * boxes
    basis_t = sample_basis.T
    model = model_prev.reshape(rows, width)
    data = samples.reshape(rows, width)
    counts = [count * boxes for count in split(gathers)]
    firsts = [sum(counts[:c]) for c in range(len(counts))]
    axes = ("gx", "gy")

    def exchange(x, mx, my):
        return swap(x, axes, mesh_shape, (mx, my))

    around = [(mx, my) for my in range(n_gy) for mx in range(0, near, 2)]
    first, second = coefficients(model, data, eval_basis, basis_t, counts)
    gather, scatter = make_tables(n_gy, near, transfer_x, transfer_y, basis_t)
    limit = threshold_map(
        support.reshape(boxes, support.shape[2]), threshold, width
    )

    parts = []
    for mx, my in around:
        part = exchange(first, mx, my) if mx or my else first
        parts += [part, exchange(part, 1, 0)]
    cuts = len(CUTS) if counts[0] % (boxes * len(CUTS)) == 0 else 1
    sums = mix_head(parts[:-1], gather)
    own_first, *far = mix_tail(sums, parts[-1], gather, cuts)
    far_first = [exchange(x, near, 0) for x in far]

    far = exchange(second, near, 0)
    parts = [second, exchange(second, 1, 0), far, exchange(far, 1, 0)]
    sums = mix_head(parts[:-1], scatter)
    own_second, *sent = mix_tail(sums, parts[-1], scatter)
    arrived = [exchange(x, mx, my) for x, (mx, my) in zip(sent, around[1:])]

    outs = ()
    outs = finish(own_second, arrived, model, data, limit, eval_basis, basis_t, firsts[1], 0, outs)
    skip = 0
    for x in far_first:
        outs = finish(own_first, [x], model, data, limit, eval_basis, basis_t, firsts[0], skip, outs)
        skip += x.shape[0]
    model_next, residual = outs
    return model_next.reshape(model_prev.shape), residual.reshape(samples.shape)


def step(mesh_shape, *args):
    return on_device(mesh_shape, *args)


def solution(mesh):
    return jax.shard_map(
        functools.partial(step, dict(mesh.shape)),
        mesh=mesh,
        in_specs=(
            P("ga", "gx", "gy", None),
            P("ga", "gx", "gy", None),
            P("gx", "gy"),
            P("gx", "gy", None),
            P(),
            P(),
            P(),
            P(),
        ),
        out_specs=(P("ga", "gx", "gy", None), P("ga", "gx", "gy", None)),
        check_vma=False,
    )
```
